32 devices in a mesh: grp: 2 (over y), ctx: 16 (over z, x, core).
Axes of the slice: x: 2, y: 2, z: 4, core: 2. Of those that a mesh axis runs over, the one named last changes fastest.
Arguments:
- query_rows: bfloat16 [4096, 4096], P(('grp', 'ctx')), parts along dimension 0, may hold values from -6 to 6
- key_rows: bfloat16 [4096, 4096], P(('grp', 'ctx')), parts along dimension 0, may hold values from -6 to 6
- value_rows: bfloat16 [4096, 4096], P(('grp', 'ctx')), parts along dimension 0, may hold values from -6 to 6
- grad_out: bfloat16 [4096, 4096], P(('grp', 'ctx')), parts along dimension 0, may hold values from -6 to 6
- conv_filter: bfloat16 [256, 128], replicated, may hold values from -0.44194174 to 0.44194174
Outputs:
- grad_query: bfloat16 [4096, 4096], P(('grp', 'ctx')), parts along dimension 0
- grad_key: bfloat16 [4096, 4096], P(('grp', 'ctx')), parts along dimension 0
- grad_value: bfloat16 [4096, 4096], P(('grp', 'ctx')), parts along dimension 0
- grad_filter: float32 [512, 128], P(('grp', 'ctx')), parts along dimension 0
The draws below stay inside these ranges and needn't reach their ends.
There are 2 independent parts, one for each index of `grp`. The reference program is written for one: setup_inputs(seed, part) draws one part's arguments, and reference() takes and returns one part's arrays. A program takes and returns all parts, laid end to end along the dimension named above; an argument that names none is the same for every part. Nothing has to cross between parts.
All inputs are finite; a program needn't handle non-finite values.
Results may differ from the reference program's by a relative error of at most 0.005.
Values may be sent and summed in bfloat16 or wider, within the bound.
No kernel may reach another device: no remote copies, remote signals or barrier semaphores. Data moves between devices by JAX's collectives and lax.ppermute only.
A program may use at most 64 MiB of HBM per device.

```python
import math
import jax
import jax.numpy as jnp
from jax import lax

D = 4096
GSIZE = 16
TAPS = 128
GROUPS = 256
TOKENS = 2048


def draw_conv_filter(key, part):
    key_base = jax.random.fold_in(key, 11)
    key_length = jax.random.fold_in(key, 12)
    raw_taps = jax.random.truncated_normal(key_base, -3.0, 3.0, (GROUPS, TAPS), jnp.float32)
    lengths = TAPS * jnp.exp(jax.random.uniform(key_length, (GROUPS, 1), jnp.float32, math.log(0.2), math.log(4.0)))
    taps_pos = jnp.arange(TAPS).astype(jnp.float32)
    decay_rows = jnp.exp(-taps_pos[None, :] / lengths)
    return (1.5 * TAPS ** (-0.5) * raw_taps * decay_rows).astype(jnp.bfloat16)


def with_spikes(result, stream_key, source, target, blocks, factor):
    owner, partner = [(jnp.arange(result.shape[dim]) // (result.shape[dim] // blocks)).reshape([-1 if axis == dim else 1 for axis in range(result.ndim)]) for dim in (source, target)]
    chosen = jax.random.permutation(stream_key, blocks)[partner]
    strong = (owner == chosen) | (owner == (partner + blocks // 2) % blocks)
    return jnp.where(strong, factor * result, result)


def block_levels(rng, dims, cuts, smallest, top_value):
    def one(position, parts):
        heights = jax.random.uniform(jax.random.fold_in(jax.random.fold_in(rng, 6), position), (parts,), jnp.float32, smallest / len(cuts), top_value / len(cuts))
        return jnp.repeat(jnp.exp(heights), dims[position] // parts).reshape((-1,) + (1,) * (len(dims) - position - 1))

    gain = one(*cuts[0])
    for cut in cuts[1:]:
        gain = gain * one(*cut)
    return gain


def noise(stream_key, dims, deviation, bound, shards=(), kind=jnp.bfloat16):
    entries = deviation * jax.random.normal(stream_key, dims, jnp.float32)
    if shards:
        entries = entries * block_levels(stream_key, dims, shards, -0.22, 0.18)
    return jnp.clip(entries, -bound, bound).astype(kind)


def noise_with(stream_key, extent, spread, limit, split, heavy, held_as=jnp.bfloat16):
    result = spread * jax.random.normal(stream_key, extent, jnp.float32)
    if split:
        result = result * block_levels(stream_key, extent, split, -0.22, 0.18)
    return jnp.clip(with_spikes(result, jax.random.fold_in(stream_key, 3), *heavy), -limit, limit).astype(held_as)


def setup_inputs(seed: int = 0, part: int = 0) -> dict:
    splits = jax.random.split(jax.random.key(seed), 6)
    part_splits = jax.random.split(jax.random.fold_in(splits[5], part), 6)
    return {
        "query_rows": noise(part_splits[0], (TOKENS, D), 1.0, 6.0, ((0, 16),)),
        "key_rows": noise(part_splits[1], (TOKENS, D), 1.0, 6.0, ((0, 16),)),
        "value_rows": noise(part_splits[2], (TOKENS, D), 1.0, 6.0, ((0, 16),)),
        "grad_out": noise_with(part_splits[3], (TOKENS, D), 1.0, 6.0, ((0, 16),), (0, 1, 16, 2.0)),
        "conv_filter": draw_conv_filter(jax.random.fold_in(splits[5], 71), part),
    }


def reference(query_rows, key_rows, value_rows, grad_out, conv_filter):
    product = (key_rows.astype(jnp.float32) * value_rows.astype(jnp.float32)).astype(jnp.bfloat16)
    gated_grad = (grad_out.astype(jnp.float32) * query_rows.astype(jnp.float32)).astype(jnp.bfloat16)
    prod_wide = product.astype(jnp.float32)
    grad_wide = gated_grad.astype(jnp.float32)
    per_channel = jnp.repeat(conv_filter.astype(jnp.float32), GSIZE, axis=0)
    padded_prod = jnp.pad(prod_wide, ((TAPS, 0), (0, 0)))
    padded_grad = jnp.pad(grad_wide, ((0, TAPS), (0, 0)))

    def tap_step(carried, index):
        mixed_sum, back_sum = carried
        weight = lax.dynamic_slice_in_dim(per_channel, index, 1, 1)[:, 0]
        shifted_prod = lax.dynamic_slice_in_dim(padded_prod, (TAPS - index).astype(jnp.int32), TOKENS, 0)
        shifted_grad = lax.dynamic_slice_in_dim(padded_grad, index, TOKENS, 0)
        mixed_sum = mixed_sum + weight[None, :] * shifted_prod
        back_sum = back_sum + weight[None, :] * shifted_grad
        column = lax.optimization_barrier(jnp.sum((grad_wide * shifted_prod).reshape(TOKENS, GROUPS, GSIZE), axis=(0, 2)))
        return ((mixed_sum, back_sum), column)
    start = (jnp.zeros((TOKENS, D), jnp.float32), jnp.zeros((TOKENS, D), jnp.float32))
    (mixed_sum, back_sum), columns = lax.scan(tap_step, start, jnp.arange(TAPS, dtype=jnp.int32))
    grad_query = (grad_out.astype(jnp.float32) * mixed_sum).astype(jnp.bfloat16)
    grad_key = (back_sum * value_rows.astype(jnp.float32)).astype(jnp.bfloat16)
    grad_value = (back_sum * key_rows.astype(jnp.float32)).astype(jnp.bfloat16)
    grad_filter = jnp.transpose(columns) / math.sqrt(TOKENS * GSIZE)
    return (grad_query, grad_key, grad_value, grad_filter)
```

```python
import math

import jax
import jax.numpy as jnp
from jax import lax
from jax.experimental import pallas as pl
from jax.experimental.pallas import tpu as pltpu
from jax.sharding import PartitionSpec as P

GSIZE = 16
B=16; LN=128; NB=8
f32=jnp.float32; bf=jnp.bfloat16
def lanes(shape): return lax.broadcasted_iota(jnp.int32, shape, 1)
def subl(shape): return lax.broadcasted_iota(jnp.int32, shape, 0)
def network(vs):
    shape=vs[0].shape
    lane=lanes(shape)
    cur=[vs[(-m)%NB] for m in range(NB)]
    for bit in (1,2,4):
        mask=(lane & (bit*16))!=0
        cur=[jnp.where(mask,cur[(m-bit)%NB],cur[m]) for m in range(NB)]
    return cur
def rot(x,s):
    s%=LN
    return x if s==0 else pltpu.roll(x,s,1)
def to_groups(tile):
    return network([rot(tile[B*a:B*a+B,:],16*a) for a in range(NB)])
def to_tokens(vs):
    es=network(vs)
    return [rot(e,-16*a) for a,e in enumerate(es)]
def unfold_back(now,bef,g):
    lane=lanes(now.shape)
    blk=((lane>>4)-g)&7
    out=[]
    for e in range(9):
        d=8-e
        if d==8: out.append(bef)
        elif d==0: out.append(now)
        else: out.append(rot(jnp.where(blk<8-d,now,bef),16*d))
    return jnp.concatenate(out,0)
def unfold_fwd(now,aft,g):
    lane=lanes(now.shape)
    blk=((lane>>4)-g)&7
    out=[]
    for d in range(9):
        if d==0: out.append(now)
        elif d==8: out.append(aft)
        else: out.append(rot(jnp.where(blk>=d,now,aft),-16*d))
    return jnp.concatenate(out,0)

def prep_kernel(h_ref,hr_ref,p_ref,g_ref,tm_ref,tb_ref,pn_ref,gn_ref,gr_ref):
    nt=p_ref.shape[1]//LN
    lane=lanes((B,LN)); row=subl((B,LN))
    def body(j,_):
        off=pl.multiple_of(j*LN,LN)
        for src,dst in ((p_ref,pn_ref),(g_ref,gn_ref)):
            tile=src[:,pl.ds(off,LN)]
            for gi,x in enumerate(to_groups(tile)):
                dst[pl.ds(pl.multiple_of((j*NB+gi)*B,B),B),:]=x
        flip=jnp.where(lanes((B,B))+subl((B,B))==B-1,1.,0.).astype(bf)
        for gi in range(NB):
            r0=pl.ds(pl.multiple_of((j*NB+gi)*B,B),B)
            gr_ref[r0,:]=jnp.dot(flip,gn_ref[r0,:],preferred_element_type=f32).astype(bf)
        hs=h_ref[pl.ds(pl.multiple_of(j*NB,NB),NB),:]
        hrs=hr_ref[pl.ds(pl.multiple_of(j*NB,NB),NB),:]
        for gi in range(NB):
            r0=pl.ds(pl.multiple_of((j*NB+gi)*B,B),B)
            rm=pltpu.roll(jnp.broadcast_to(hrs[gi:gi+1,:],(B,LN)),1,1,stride=1,stride_axis=0)
            tm_ref[r0,0:LN]=jnp.where(lane>row,rm,0.).astype(bf)
            tm_ref[r0,LN:2*LN]=jnp.where(lane<=row,rm,0.).astype(bf)
            rb=pltpu.roll(jnp.broadcast_to(hs[gi:gi+1,:],(B,LN)),0,1,stride=1,stride_axis=0)
            tb_ref[r0,0:LN]=jnp.where(lane>=row,rb,0.).astype(bf)
            tb_ref[r0,LN:2*LN]=jnp.where(lane<row,rb,0.).astype(bf)
        return 0
    lax.fori_loop(0,nt,body,0)

def mixed_kernel(tm_ref,pn_ref,gr_ref,bef_ref,go_ref,gq_ref,f_ref):
    nt=bef_ref.shape[1]//LN
    lane=lanes((B,LN)); row=subl((B,LN))
    def body(j,_):
        off=pl.multiple_of(j*LN,LN)
        bef=to_groups(bef_ref[:,pl.ds(off,LN)])
        ys=[];fr=[]
        for gi in range(NB):
            r0=pl.ds(pl.multiple_of((j*NB+gi)*B,B),B)
            xu=unfold_back(pn_ref[r0,:],bef[gi],gi)
            ys.append(jnp.dot(tm_ref[r0,0:9*B],xu,preferred_element_type=f32))
            F=lax.dot_general(gr_ref[r0,:],xu,(((1,),(1,)),((),())),preferred_element_type=f32)
            F2=jnp.concatenate([F[:,LN:LN+B],jnp.zeros((B,LN-B),f32)],1)
            C=jnp.where(lane+row<=B-1,F2,F[:,:LN])
            fr.append(jnp.sum(pltpu.roll(C,LN-B,1,stride=1,stride_axis=0),0,keepdims=True))
        f_ref[pl.ds(pl.multiple_of(j*NB,NB),NB),:]=jnp.concatenate(fr,0)
        for a,y in enumerate(to_tokens(ys)):
            go=go_ref[B*a:B*a+B,pl.ds(off,LN)].astype(f32)
            gq_ref[B*a:B*a+B,pl.ds(off,LN)]=(go*y).astype(bf)
        return 0
    lax.fori_loop(0,nt,body,0)

def back_kernel(tb_ref,gn_ref,aft_ref,k_ref,v_ref,gk_ref,gv_ref):
    nt=aft_ref.shape[1]//LN
    def body(j,_):
        off=pl.multiple_of(j*LN,LN)
        aft=to_groups(aft_ref[:,pl.ds(off,LN)])
        ys=[]
        for gi in range(NB):
            r0=pl.ds(pl.multiple_of((j*NB+gi)*B,B),B)
            xu=unfold_fwd(gn_ref[r0,:],aft[gi],gi)
            ys.append(jnp.dot(tb_ref[r0,0:9*B],xu,preferred_element_type=f32))
        for a,y in enumerate(to_tokens(ys)):
            sl=(slice(B*a,B*a+B),pl.ds(off,LN))
            gk_ref[sl]=(v_ref[sl].astype(f32)*y).astype(bf)
            gv_ref[sl]=(k_ref[sl].astype(f32)*y).astype(bf)
        return 0
    lax.fori_loop(0,nt,body,0)

V=pl.BlockSpec(memory_space=pltpu.VMEM)
def prep(h,hr,p,g):
    G=h.shape[0]; S=jax.ShapeDtypeStruct
    return pl.pallas_call(prep_kernel,out_shape=(S((G*B,2*LN),bf),S((G*B,2*LN),bf),S((G*B,LN),bf),S((G*B,LN),bf),S((G*B,LN),bf)),
        in_specs=[V]*4,out_specs=(V,)*5,name="prep")(h,hr,p,g)
def mixed(tm,pn,gn,bef,go):
    S=jax.ShapeDtypeStruct
    return pl.pallas_call(mixed_kernel,out_shape=(S(go.shape,bf),S((tm.shape[0]//B,LN),f32)),in_specs=[V]*5,out_specs=(V,)*2,name="mixed")(tm,pn,gn,bef,go)
def back(tb,gn,aft,k,v):
    S=jax.ShapeDtypeStruct
    return pl.pallas_call(back_kernel,out_shape=(S(k.shape,bf),S(k.shape,bf)),in_specs=[V]*5,out_specs=(V,)*2,name="back")(tb,gn,aft,k,v)


def reduce_filter(partial, size):
    index = lax.axis_index("ctx")
    step = 1
    pieces = partial.reshape((size, partial.shape[0] // size) + partial.shape[1:])
    while step < size:
        pairs = [(i, i ^ step) for i in range(size)]
        split = pieces.reshape((pieces.shape[0] // 2, 2) + pieces.shape[1:])
        bit = (index // step) % 2
        keep = lax.dynamic_index_in_dim(split, bit, 1, keepdims=False)
        send = lax.dynamic_index_in_dim(split, 1 - bit, 1, keepdims=False)
        pieces = keep + lax.ppermute(send, "ctx", pairs)
        step *= 2
    return pieces[0]


def shards(query_rows, key_rows, value_rows, grad_out, conv_filter):
    size = lax.axis_size("ctx")
    product = (key_rows.astype(f32) * value_rows.astype(f32)).astype(bf)
    gated = (grad_out.astype(f32) * query_rows.astype(f32)).astype(bf)
    before = lax.ppermute(product, "ctx", [(i, i + 1) for i in range(size - 1)])
    after = lax.ppermute(gated, "ctx", [(i + 1, i) for i in range(size - 1)])
    taps = conv_filter.astype(f32)
    tm, tb, pn, gn, gr = prep(taps, taps[:, ::-1], product, gated)
    grad_query, partial = mixed(tm, pn, gr, before, grad_out)
    own = reduce_filter(partial, size)
    grad_key, grad_value = back(tb, gn, after, key_rows, value_rows)
    scale = 1.0 / math.sqrt(query_rows.shape[0] * size * GSIZE)
    return grad_query, grad_key, grad_value, own[:, ::-1] * scale


def solution(mesh):
    rows = P(("grp", "ctx"), None)
    return jax.shard_map(
        shards,
        mesh=mesh,
        in_specs=(rows, rows, rows, rows, P()),
        out_specs=(rows, rows, rows, rows),
        check_vma=False,
    )
```

```python
import math

import jax
import jax.numpy as jnp
from jax import lax
from jax.experimental import pallas as pl
from jax.experimental.pallas import tpu as pltpu
from jax.sharding import PartitionSpec as P

GSIZE = 16
B=32; LN=128; NB=LN//B; LB=LN//NB; SG=LB//GSIZE; H=16
f32=jnp.float32; bf=jnp.bfloat16
def lanes(shape): return lax.broadcasted_iota(jnp.int32, shape, 1)
def subl(shape): return lax.broadcasted_iota(jnp.int32, shape, 0)
def network(vs):
    lane=lanes(vs[0].shape)
    cur=[vs[(-m)%NB] for m in range(NB)]
    bit=1
    while bit<NB:
        mask=(lane & (bit*LB))!=0
        cur=[jnp.where(mask,cur[(m-bit)%NB],cur[m]) for m in range(NB)]
        bit*=2
    return cur
def rot(x,s):
    s%=LN
    return x if s==0 else pltpu.roll(x,s,1)
def to_groups(tile):
    return network([rot(tile[B*a:B*a+B,:],LB*a) for a in range(NB)])
def to_tokens(vs):
    return [rot(e,-LB*a) for a,e in enumerate(network(vs))]
def place(shape,s):
    return (lanes(shape)//LB-s)&(NB-1)
def unfold_back(now,bef,s):
    blk=place(now.shape,s)
    return jnp.concatenate([bef]+[rot(jnp.where(blk<NB-d,now,bef),LB*d) for d in range(NB-1,0,-1)]+[now],0)
def unfold_fwd(now,aft,s):
    blk=place(now.shape,s)
    return jnp.concatenate([now]+[rot(jnp.where(blk>=d,now,aft),-LB*d) for d in range(1,NB)]+[aft],0)
def pick(out,half):
    lane=lanes((B,LN))
    y=out[half*SG*B:half*SG*B+B,half*LN:half*LN+LN]
    for q in range(1,SG):
        y=jnp.where((lane//GSIZE)%SG==q,out[(half*SG+q)*B:(half*SG+q+1)*B,half*LN:half*LN+LN],y)
    return y

def prep_kernel(h_ref,hr_ref,g_ref,tm_ref,tb_ref,gr_ref):
    nt=g_ref.shape[1]//LN
    gt=LN//GSIZE
    lane=lanes((B,LN)); row=subl((B,LN))
    flip=jnp.where(lanes((H,H))+subl((H,H))==H-1,1.,0.).astype(bf)
    lane16=(lanes((H,LN))//GSIZE)%SG
    for j in range(nt):
        gs=to_groups(g_ref[:,j*LN:(j+1)*LN])
        for s in range(NB):
            for half in range(B//H):
                x=jnp.dot(flip,gs[s][half*H:(half+1)*H],preferred_element_type=f32)
                for q in range(SG):
                    r=((j*NB+s)*SG+q)*H
                    gr_ref[r:r+H,half*LN:(half+1)*LN]=jnp.where(lane16==q,x,0.).astype(bf)
        for gi in range(gt):
            g=j*gt+gi
            r0=slice(g*B,(g+1)*B)
            rm=pltpu.roll(jnp.broadcast_to(hr_ref[g:g+1,:],(B,LN)),1,1,stride=1,stride_axis=0)
            tm_ref[r0,0:LN]=jnp.where(lane>row,rm,0.).astype(bf)
            tm_ref[r0,LN:2*LN]=jnp.where(lane<=row,rm,0.).astype(bf)
            rb=pltpu.roll(jnp.broadcast_to(h_ref[g:g+1,:],(B,LN)),0,1,stride=1,stride_axis=0)
            tb_ref[r0,0:LN]=jnp.where(lane>=row,rb,0.).astype(bf)
            tb_ref[r0,LN:2*LN]=jnp.where(lane<row,rb,0.).astype(bf)

def mixed_kernel(tm_ref,p_ref,gr_ref,bef_ref,go_ref,gq_ref,f_ref):
    nt=bef_ref.shape[1]//LN
    gt=LN//GSIZE
    lane=lanes((H,LN)); row=subl((H,LN))
    for j in range(nt):
        co=slice(j*LN,(j+1)*LN)
        now=to_groups(p_ref[:,co]); bef=to_groups(bef_ref[:,co])
        ys=[];fr=[]
        for s in range(0,NB,2):
            us=[unfold_back(now[s+i],bef[s+i],s+i) for i in (0,1)]
            r=(j*gt+s*SG)*B
            y=jnp.dot(tm_ref[r:r+2*SG*B,0:LN+B],jnp.concatenate(us,1),preferred_element_type=f32)
            ys+=[pick(y,0),pick(y,1)]
            for i in (0,1):
                r=(j*gt+(s+i)*SG)*H
                xu=us[i]
                if B==H: rhs=xu
                else: rhs=jnp.concatenate([xu[0:LN+H],xu[H:LN+2*H]],1)
                FF=lax.dot_general(gr_ref[r:r+SG*H,:],rhs,(((1,),(1,)),((),())),preferred_element_type=f32)
                for q in range(SG):
                    F=FF[q*H:(q+1)*H]
                    F2=jnp.concatenate([F[:,LN:LN+H],jnp.zeros((H,LN-H),f32)],1)
                    C=jnp.where(lane+row<=H-1,F2,F[:,:LN])
                    fr.append(jnp.sum(pltpu.roll(C,LN-H,1,stride=1,stride_axis=0),0,keepdims=True))
        f_ref[j*gt:(j+1)*gt,:]=jnp.concatenate(fr,0)
        for a,y in enumerate(to_tokens(ys)):
            gq_ref[B*a:B*a+B,co]=(go_ref[B*a:B*a+B,co].astype(f32)*y).astype(bf)

def back_kernel(tb_ref,g_ref,aft_ref,k_ref,v_ref,gk_ref,gv_ref):
    nt=aft_ref.shape[1]//LN
    gt=LN//GSIZE
    for j in range(nt):
        co=slice(j*LN,(j+1)*LN)
        now=to_groups(g_ref[:,co]); aft=to_groups(aft_ref[:,co])
        ys=[]
        for s in range(0,NB,2):
            xu=jnp.concatenate([unfold_fwd(now[s+i],aft[s+i],s+i) for i in (0,1)],1)
            r=(j*gt+s*SG)*B
            y=jnp.dot(tb_ref[r:r+2*SG*B,0:LN+B],xu,preferred_element_type=f32)
            ys+=[pick(y,0),pick(y,1)]
        for a,y in enumerate(to_tokens(ys)):
            sl=(slice(B*a,B*a+B),co)
            gk_ref[sl]=(v_ref[sl].astype(f32)*y).astype(bf)
            gv_ref[sl]=(k_ref[sl].astype(f32)*y).astype(bf)

STEP=1024
def specs(rows,channels):
    n=channels//STEP
    tok=pl.BlockSpec((rows,STEP),lambda i:(0,i))
    tab=pl.BlockSpec((STEP//GSIZE*B,2*LN),lambda i:(i,0))
    rev=pl.BlockSpec((STEP//GSIZE*H,2*LN),lambda i:(i,0))
    filt=pl.BlockSpec((STEP//GSIZE,LN),lambda i:(i,0))
    return n,tok,tab,filt,rev
def prep(h,hr,g):
    S=jax.ShapeDtypeStruct; G=h.shape[0]
    n,tok,tab,filt,rev=specs(*g.shape)
    t=S((G*B,2*LN),bf)
    return pl.pallas_call(prep_kernel,out_shape=(t,t,S((G*H,2*LN),bf)),grid=(n,),in_specs=[filt,filt,tok],out_specs=(tab,tab,rev),name="prep")(h,hr,g)
def mixed(tm,p,gr,bef,go):
    S=jax.ShapeDtypeStruct
    n,tok,tab,filt,rev=specs(*go.shape)
    return pl.pallas_call(mixed_kernel,out_shape=(S(go.shape,bf),S((tm.shape[0]//B,LN),f32)),grid=(n,),in_specs=[tab,tok,rev,tok,tok],out_specs=(tok,filt),name="mixed")(tm,p,gr,bef,go)
def back(tb,g,aft,k,v):
    S=jax.ShapeDtypeStruct
    n,tok,tab,filt,rev=specs(*k.shape)
    return pl.pallas_call(back_kernel,out_shape=(S(k.shape,bf),S(k.shape,bf)),grid=(n,),in_specs=[tab]+[tok]*4,out_specs=(tok,)*2,name="back")(tb,g,aft,k,v)


def reduce_filter(partial, size):
    index = lax.axis_index("ctx")
    step = 1
    pieces = partial.reshape((size, partial.shape[0] // size) + partial.shape[1:])
    while step < size:
        pairs = [(i, i ^ step) for i in range(size)]
        split = pieces.reshape((pieces.shape[0] // 2, 2) + pieces.shape[1:])
        bit = (index // step) % 2
        keep = lax.dynamic_index_in_dim(split, bit, 1, keepdims=False)
        send = lax.dynamic_index_in_dim(split, 1 - bit, 1, keepdims=False)
        pieces = keep + lax.ppermute(send, "ctx", pairs)
        step *= 2
    return pieces[0]


def shards(query_rows, key_rows, value_rows, grad_out, conv_filter):
    size = lax.axis_size("ctx")
    product = (key_rows.astype(f32) * value_rows.astype(f32)).astype(bf)
    gated = (grad_out.astype(f32) * query_rows.astype(f32)).astype(bf)
    before = lax.ppermute(product, "ctx", [(i, i + 1) for i in range(size - 1)])
    after = lax.ppermute(gated, "ctx", [(i + 1, i) for i in range(size - 1)])
    taps = conv_filter.astype(f32)
    tm, tb, gr = prep(taps, taps[:, ::-1], gated)
    grad_query, partial = mixed(tm, product, gr, before, grad_out)
    own = reduce_filter(partial, size)
    grad_key, grad_value = back(tb, gated, after, key_rows, value_rows)
    scale = 1.0 / math.sqrt(query_rows.shape[0] * size * GSIZE)
    return grad_query, grad_key, grad_value, own[:, ::-1] * scale


def solution(mesh):
    rows = P(("grp", "ctx"), None)
    return jax.shard_map(
        shards,
        mesh=mesh,
        in_specs=(rows, rows, rows, rows, P()),
        out_specs=(rows, rows, rows, rows),
        check_vma=False,
    )
```

```python
import math

import jax
import jax.numpy as jnp
from jax import lax
from jax.experimental import pallas as pl
from jax.experimental.pallas import tpu as pltpu
from jax.sharding import PartitionSpec as P

GSIZE = 16
f32 = jnp.float32
bf = jnp.bfloat16
LN = 128
B = 32
NB = LN // B
LB = LN // NB
SG = LB // GSIZE
GT = LN // GSIZE
H = 16
STEP = 1024


def lanes(shape):
    return lax.broadcasted_iota(jnp.int32, shape, 1)


def subl(shape):
    return lax.broadcasted_iota(jnp.int32, shape, 0)


def network(vs):
    lane = lanes(vs[0].shape)
    cur = [vs[(-m) % NB] for m in range(NB)]
    bit = 1
    while bit < NB:
        mask = (lane & (bit * LB)) != 0
        cur = [jnp.where(mask, cur[(m - bit) % NB], cur[m]) for m in range(NB)]
        bit *= 2
    return cur


def rot(x, s):
    s %= LN
    return x if s == 0 else pltpu.roll(x, s, 1)


def to_groups(tile):
    return network([rot(tile[B * a : B * a + B, :], LB * a) for a in range(NB)])


def to_tokens(vs):
    return [rot(e, -LB * a) for a, e in enumerate(network(vs))]


def place(shape, s):
    return (lanes(shape) // LB - s) & (NB - 1)


def unfold_back(now, bef, s):
    blk = place(now.shape, s)
    mid = [rot(jnp.where(blk < NB - d, now, bef), LB * d) for d in range(NB - 1, 0, -1)]
    return jnp.concatenate([bef] + mid + [now], 0)


def unfold_fwd(now, aft, s):
    blk = place(now.shape, s)
    mid = [rot(jnp.where(blk >= d, now, aft), -LB * d) for d in range(1, NB)]
    return jnp.concatenate([now] + mid + [aft], 0)


def pick(out, half):
    lane = lanes((B, LN))
    y = out[half * SG * B : half * SG * B + B, half * LN : half * LN + LN]
    for q in range(1, SG):
        other = out[(half * SG + q) * B : (half * SG + q + 1) * B, half * LN : half * LN + LN]
        y = jnp.where((lane // GSIZE) % SG == q, other, y)
    return y


def column_sums(vs):
    row = subl(vs[0].shape)
    bit = 1
    while len(vs) > 1:
        low = (row & bit) == 0
        vs = [
            jnp.where(low, a, b) + pltpu.roll(jnp.where(low, b, a), 8 - bit, 0)
            for a, b in zip(vs[0::2], vs[1::2])
        ]
        bit *= 2
    return vs[0]


def prep_kernel(h_ref, k_ref, v_ref, p_ref, pn_ref, pr_ref, tm_ref, tb_ref):
    nt = k_ref.shape[1] // LN
    flip = jnp.where(lanes((H, H)) + subl((H, H)) == H - 1, 1.0, 0.0).astype(bf)
    turn = jnp.where(lanes((LN, LN)) + subl((LN, LN)) == LN - 1, 1.0, 0.0).astype(bf)
    h = h_ref[...].astype(f32)
    hr = jnp.dot(h_ref[...], turn, preferred_element_type=f32)
    for j in range(nt):
        co = slice(j * LN, (j + 1) * LN)
        p = (k_ref[:, co].astype(f32) * v_ref[:, co].astype(f32)).astype(bf)
        p_ref[:, co] = p
        ps = to_groups(p)
        for s in range(NB):
            r = (j * NB + s) * B
            pn_ref[r : r + B, :] = ps[s]
            for at in range(0, B, H):
                x = jnp.dot(flip, ps[s][at : at + H], preferred_element_type=f32)
                pr_ref[r + at : r + at + H, :] = x.astype(bf)
        for g in range(j * GT, (j + 1) * GT):
            r0 = slice(g * B, (g + 1) * B)
            rm = jnp.broadcast_to(hr[g : g + 1, :], (B, LN))
            tm_ref[r0, :] = pltpu.roll(rm, 1, 1, stride=1, stride_axis=0).astype(bf)
            rb = jnp.broadcast_to(h[g : g + 1, :], (B, LN))
            tb_ref[r0, :] = pltpu.roll(rb, 0, 1, stride=1, stride_axis=0).astype(bf)


def taps_of(ring, first):
    out = []
    for x in (ring[i : i + B] for i in range(0, ring.shape[0], B)):
        inside = lanes(x.shape) > subl(x.shape) if first else lanes(x.shape) >= subl(x.shape)
        zero = jnp.zeros_like(x)
        out.append(jnp.concatenate([jnp.where(inside, x, zero), jnp.where(inside, zero, x)[:, :B]], 1))
    return jnp.concatenate(out, 0)


def mixed_kernel(t_ref, pn_ref, bef_ref, go_ref, *rest):
    gq_ref = rest[-1]
    nt = bef_ref.shape[1] // LN
    for j in range(nt):
        co = slice(j * LN, (j + 1) * LN)
        bef = to_groups(bef_ref[:, co])
        ys = []
        for s in range(0, NB, 2):
            us = []
            for i in (0, 1):
                r = (j * NB + s + i) * B
                us.append(unfold_back(pn_ref[r : r + B, :], bef[s + i], s + i))
            r = (j * GT + s * SG) * B
            t = taps_of(t_ref[r : r + 2 * SG * B, :], True)
            y = jnp.dot(t, jnp.concatenate(us, 1), preferred_element_type=f32)
            ys += [pick(y, 0), pick(y, 1)]
        for a, y in enumerate(to_tokens(ys)):
            rows = slice(B * a, B * a + B)
            gq_ref[rows, co] = (go_ref[rows, co].astype(f32) * y).astype(bf)


def back_kernel(t_ref, pr_ref, g_ref, aft_ref, k_ref, v_ref, *rest):
    gk_ref, gv_ref, f_ref = rest[-3:]
    nt = aft_ref.shape[1] // LN
    lane, row = lanes((H, LN)), subl((H, LN))
    for j in range(nt):
        co = slice(j * LN, (j + 1) * LN)
        now, aft = to_groups(g_ref[:, co]), to_groups(aft_ref[:, co])
        ys, sums = [], []
        for s in range(0, NB, 2):
            us = [unfold_fwd(now[s + i], aft[s + i], s + i) for i in (0, 1)]
            r = (j * GT + s * SG) * B
            t = taps_of(t_ref[r : r + 2 * SG * B, :], False)
            y = jnp.dot(t, jnp.concatenate(us, 1), preferred_element_type=f32)
            ys += [pick(y, 0), pick(y, 1)]
            for i in (0, 1):
                r = (j * NB + s + i) * B
                rhs = jnp.concatenate([us[i][0 : LN + H], us[i][H : LN + 2 * H]], 1)
                own = jnp.concatenate([pr_ref[r : r + H, :], pr_ref[r + H : r + B, :]], 1)
                part = (lanes(own.shape) // GSIZE) % SG
                lhs = jnp.concatenate([jnp.where(part == q, own, jnp.zeros_like(own)) for q in range(SG)], 0)
                both = lax.dot_general(
                    lhs, rhs, (((1,), (1,)), ((), ())), preferred_element_type=f32
                )
                for q in range(SG):
                    f = both[q * H : (q + 1) * H]
                    edge = jnp.concatenate([f[:, LN : LN + H], jnp.zeros((H, LN - H), f32)], 1)
                    c = jnp.where(lane + row < H - 1, edge, f[:, :LN])
                    c = pltpu.roll(c, LN - H + 1, 1, stride=1, stride_axis=0)
                    sums.append(c[:8] + c[8:])
        f_ref[j * GT : (j + 1) * GT, :] = column_sums(sums)
        for a, y in enumerate(to_tokens(ys)):
            sl = (slice(B * a, B * a + B), co)
            gk_ref[sl] = (v_ref[sl].astype(f32) * y).astype(bf)
            gv_ref[sl] = (k_ref[sl].astype(f32) * y).astype(bf)


def hbm(x):
    return pltpu.with_memory_space_constraint(x, pltpu.HBM)


def tok(start=0):
    return pl.BlockSpec((LN, STEP), lambda i: (0, i + start))


def table(rows, start=0):
    return pl.BlockSpec((STEP // GSIZE * rows, LN), lambda i: (i + start, 0))


def shape(*dims, kind=bf):
    return jax.ShapeDtypeStruct(dims, kind)


def prep(h, k, v):
    groups = h.shape[0]
    t, r = shape(groups * B, LN), shape(groups * H, LN)
    return pl.pallas_call(
        prep_kernel,
        out_shape=(shape(*k.shape), r, r, t, t),
        grid=(k.shape[1] // STEP,),
        in_specs=[table(1), tok(), tok()],
        out_specs=(tok(), table(H), table(H), table(B), table(B)),
        name="prep",
    )(hbm(h), hbm(k), hbm(v))


ANY = pl.BlockSpec(memory_space=pl.ANY)
PARAMS = pltpu.CompilerParams(vmem_limit_bytes=48 << 20)


def mixed(t, pn, bef, go, start, old):
    at = start // STEP
    return pl.pallas_call(
        mixed_kernel,
        out_shape=(shape(*go.shape),),
        grid=(bef.shape[1] // STEP,),
        in_specs=[table(B, at), table(H, at), tok(), tok(at)] + [ANY] * len(old),
        out_specs=(tok(at),),
        input_output_aliases={4 + i: i for i in range(len(old))},
        compiler_params=PARAMS,
        name="mixed",
    )(*(hbm(x) for x in (t, pn)), bef, hbm(go), *old)


def back(t, pr, g, aft, k, v, start, old):
    at = start // STEP
    return pl.pallas_call(
        back_kernel,
        out_shape=(shape(*k.shape), shape(*k.shape), shape(k.shape[1] // GSIZE, LN, kind=f32)),
        grid=(g.shape[1] // STEP,),
        in_specs=[table(B, at), table(H, at), tok(), tok(), tok(at), tok(at)] + [ANY] * len(old),
        out_specs=(tok(at), tok(at), table(1, at)),
        input_output_aliases={6 + i: i for i in range(len(old))},
        compiler_params=PARAMS,
        name="back",
    )(hbm(t), hbm(pr), hbm(g), aft, hbm(k), hbm(v), *old)


def pairs_of(size, step):
    return [(i, i ^ step) for i in range(size)]


def reduce_filter(partial, size):
    index = lax.axis_index("ctx")
    step = 1
    pieces = partial.reshape((size, partial.shape[0] // size) + partial.shape[1:])
    while step < size:
        split = pieces.reshape((pieces.shape[0] // 2, 2) + pieces.shape[1:])
        bit = (index // step) % 2
        keep = lax.dynamic_index_in_dim(split, bit, 1, keepdims=False)
        send = lax.dynamic_index_in_dim(split, 1 - bit, 1, keepdims=False)
        got = lax.ppermute(send, "ctx", pairs_of(size, step))
        pieces = keep + got
        step *= 2
    return pieces[0]


PARTS = 2


def shards(query_rows, key_rows, value_rows, grad_out, conv_filter):
    size = lax.axis_size("ctx")
    channels = key_rows.shape[1]
    width = channels // PARTS
    down = [(i + 1, i) for i in range(size - 1)]
    up = [(i, i + 1) for i in range(size - 1)]
    gated, after = [], []
    for c in range(PARTS):
        cut = slice(c * width, (c + 1) * width)
        gated.append((grad_out[:, cut].astype(f32) * query_rows[:, cut].astype(f32)).astype(bf))
        after.append(lax.ppermute(gated[c], "ctx", down))
    product, pn, pr, tm, tb = prep(conv_filter, key_rows, value_rows)
    before = lax.ppermute(product, "ctx", up)
    old = ()
    for c in range(PARTS):
        old = back(tb, pr, gated[c], after[c], key_rows, value_rows, c * width, old)
    grad_key, grad_value, partial = old
    own = reduce_filter(partial, size)
    (grad_query,) = mixed(tm, pn, before, grad_out, 0, ())
    scale = 1.0 / math.sqrt(query_rows.shape[0] * size * GSIZE)
    return grad_query, grad_key, grad_value, own * scale


def solution(mesh):
    rows = P(("grp", "ctx"), None)

    return jax.shard_map(
        shards,
        mesh=mesh,
        in_specs=(rows, rows, rows, rows, P()),
        out_specs=(rows, rows, rows, rows),
        check_vma=False,
    )
```

```python
import math

import jax
import jax.numpy as jnp
from jax import lax
from jax.experimental import pallas as pl
from jax.experimental.pallas import tpu as pltpu
from jax.sharding import PartitionSpec as P

GSIZE = 16
f32 = jnp.float32
bf = jnp.bfloat16
LN = 128
B = 32
NB = LN // B
LB = LN // NB
SG = LB // GSIZE
GT = LN // GSIZE
H = 16
STEP = 1024


def lanes(shape):
    return lax.broadcasted_iota(jnp.int32, shape, 1)


def subl(shape):
    return lax.broadcasted_iota(jnp.int32, shape, 0)


def network(vs):
    lane = lanes(vs[0].shape)
    cur = [vs[(-m) % NB] for m in range(NB)]
    bit = 1
    while bit < NB:
        mask = (lane & (bit * LB)) != 0
        cur = [jnp.where(mask, cur[(m - bit) % NB], cur[m]) for m in range(NB)]
        bit *= 2
    return cur


def rot(x, s):
    s %= LN
    return x if s == 0 else pltpu.roll(x, s, 1)


def to_groups(tile):
    return network([rot(tile[B * a : B * a + B, :], LB * a) for a in range(NB)])


def to_tokens(vs):
    return [rot(e, -LB * a) for a, e in enumerate(network(vs))]


def place(shape, s):
    return (lanes(shape) // LB - s) & (NB - 1)


def unfold_back(now, bef, s):
    blk = place(now.shape, s)
    mid = [rot(jnp.where(blk < NB - d, now, bef), LB * d) for d in range(NB - 1, 0, -1)]
    return jnp.concatenate([bef] + mid + [now], 0)


def unfold_fwd(now, aft, s):
    blk = place(now.shape, s)
    mid = [rot(jnp.where(blk >= d, now, aft), -LB * d) for d in range(1, NB)]
    return jnp.concatenate([now] + mid + [aft], 0)


def pick(out, half):
    lane = lanes((B, LN))
    y = out[half * SG * B : half * SG * B + B, half * LN : half * LN + LN]
    for q in range(1, SG):
        other = out[(half * SG + q) * B : (half * SG + q + 1) * B, half * LN : half * LN + LN]
        y = jnp.where((lane // GSIZE) % SG == q, other, y)
    return y


def column_sums(vs):
    row = subl(vs[0].shape)
    bit = 1
    while len(vs) > 1:
        low = (row & bit) == 0
        vs = [
            jnp.where(low, a, b) + pltpu.roll(jnp.where(low, b, a), 8 - bit, 0)
            for a, b in zip(vs[0::2], vs[1::2])
        ]
        bit *= 2
    return vs[0]


def prep_kernel(h_ref, k_ref, v_ref, p_ref, pn_ref, pr_ref, tm_ref, tb_ref):
    nt = k_ref.shape[1] // LN
    flip = jnp.where(lanes((H, H)) + subl((H, H)) == H - 1, 1.0, 0.0).astype(bf)
    turn = jnp.where(lanes((LN, LN)) + subl((LN, LN)) == LN - 1, 1.0, 0.0).astype(bf)
    h = h_ref[...].astype(f32)
    hr = jnp.dot(h_ref[...], turn, preferred_element_type=f32)
    for j in range(nt):
        co = slice(j * LN, (j + 1) * LN)
        p = (k_ref[:, co].astype(f32) * v_ref[:, co].astype(f32)).astype(bf)
        p_ref[:, co] = p
        ps = to_groups(p)
        for s in range(NB):
            r = (j * NB + s) * B
            pn_ref[r : r + B, :] = ps[s]
            for at in range(0, B, H):
                x = jnp.dot(flip, ps[s][at : at + H], preferred_element_type=f32)
                pr_ref[r + at : r + at + H, :] = x.astype(bf)
        for g in range(j * GT, (j + 1) * GT):
            r0 = slice(g * B, (g + 1) * B)
            rm = jnp.broadcast_to(hr[g : g + 1, :], (B, LN))
            tm_ref[r0, :] = pltpu.roll(rm, 1, 1, stride=1, stride_axis=0).astype(bf)
            rb = jnp.broadcast_to(h[g : g + 1, :], (B, LN))
            tb_ref[r0, :] = pltpu.roll(rb, 0, 1, stride=1, stride_axis=0).astype(bf)


def taps_of(ring, first):
    out = []
    for x in (ring[i : i + B] for i in range(0, ring.shape[0], B)):
        inside = lanes(x.shape) > subl(x.shape) if first else lanes(x.shape) >= subl(x.shape)
        zero = jnp.zeros_like(x)
        out.append(jnp.concatenate([jnp.where(inside, x, zero), jnp.where(inside, zero, x)[:, :B]], 1))
    return jnp.concatenate(out, 0)


def mixed_kernel(t_ref, pn_ref, bef_ref, go_ref, *rest):
    gq_ref = rest[-1]
    nt = bef_ref.shape[1] // LN
    for j in range(nt):
        co = slice(j * LN, (j + 1) * LN)
        bef = to_groups(bef_ref[:, co])
        ys = []
        for s in range(0, NB, 2):
            us = []
            for i in (0, 1):
                r = (j * NB + s + i) * B
                us.append(unfold_back(pn_ref[r : r + B, :], bef[s + i], s + i))
            r = (j * GT + s * SG) * B
            t = taps_of(t_ref[r : r + 2 * SG * B, :], True)
            y = jnp.dot(t, jnp.concatenate(us, 1), preferred_element_type=f32)
            ys += [pick(y, 0), pick(y, 1)]
        for a, y in enumerate(to_tokens(ys)):
            rows = slice(B * a, B * a + B)
            gq_ref[rows, co] = (go_ref[rows, co].astype(f32) * y).astype(bf)


def back_kernel(t_ref, pr_ref, g_ref, aft_ref, k_ref, v_ref, *rest):
    gk_ref, gv_ref, f_ref = rest[-3:]
    nt = aft_ref.shape[1] // LN
    lane, row = lanes((H, LN)), subl((H, LN))
    for j in range(nt):
        co = slice(j * LN, (j + 1) * LN)
        now, aft = to_groups(g_ref[:, co]), to_groups(aft_ref[:, co])
        ys, sums = [], []
        for s in range(0, NB, 2):
            us = [unfold_fwd(now[s + i], aft[s + i], s + i) for i in (0, 1)]
            r = (j * GT + s * SG) * B
            t = taps_of(t_ref[r : r + 2 * SG * B, :], False)
            y = jnp.dot(t, jnp.concatenate(us, 1), preferred_element_type=f32)
            ys += [pick(y, 0), pick(y, 1)]
            for i in (0, 1):
                r = (j * NB + s + i) * B
                rhs = jnp.concatenate([us[i][0 : LN + H], us[i][H : LN + 2 * H]], 1)
                own = jnp.concatenate([pr_ref[r : r + H, :], pr_ref[r + H : r + B, :]], 1)
                part = (lanes(own.shape) // GSIZE) % SG
                lhs = jnp.concatenate([jnp.where(part == q, own, jnp.zeros_like(own)) for q in range(SG)], 0)
                both = lax.dot_general(
                    lhs, rhs, (((1,), (1,)), ((), ())), preferred_element_type=f32
                )
                for q in range(SG):
                    f = both[q * H : (q + 1) * H]
                    edge = jnp.concatenate([f[:, LN : LN + H], jnp.zeros((H, LN - H), f32)], 1)
                    c = jnp.where(lane + row < H - 1, edge, f[:, :LN])
                    c = pltpu.roll(c, LN - H + 1, 1, stride=1, stride_axis=0)
                    sums.append(c[:8] + c[8:])
        f_ref[j * GT : (j + 1) * GT, :] = column_sums(sums)
        for a, y in enumerate(to_tokens(ys)):
            sl = (slice(B * a, B * a + B), co)
            gk_ref[sl] = (v_ref[sl].astype(f32) * y).astype(bf)
            gv_ref[sl] = (k_ref[sl].astype(f32) * y).astype(bf)


def hbm(x):
    return pltpu.with_memory_space_constraint(x, pltpu.HBM)


def tok(start=0):
    return pl.BlockSpec((LN, STEP), lambda i: (0, i + start))


def table(rows, start=0):
    return pl.BlockSpec((STEP // GSIZE * rows, LN), lambda i: (i + start, 0))


def shape(*dims, kind=bf):
    return jax.ShapeDtypeStruct(dims, kind)


def prep(h, k, v):
    groups = h.shape[0]
    t, r = shape(groups * B, LN), shape(groups * H, LN)
    return pl.pallas_call(
        prep_kernel,
        out_shape=(shape(*k.shape), r, r, t, t),
        grid=(k.shape[1] // STEP,),
        in_specs=[table(1), tok(), tok()],
        out_specs=(tok(), table(H), table(H), table(B), table(B)),
        name="prep",
    )(hbm(h), hbm(k), hbm(v))


ANY = pl.BlockSpec(memory_space=pl.ANY)
PARAMS = pltpu.CompilerParams(vmem_limit_bytes=48 << 20)


def mixed(t, pn, bef, go, start, old):
    at = start // STEP
    return pl.pallas_call(
        mixed_kernel,
        out_shape=(shape(*go.shape),),
        grid=(bef.shape[1] // STEP,),
        in_specs=[table(B, at), table(H, at), tok(), tok(at)] + [ANY] * len(old),
        out_specs=(tok(at),),
        input_output_aliases={4 + i: i for i in range(len(old))},
        compiler_params=PARAMS,
        name="mixed",
    )(*(hbm(x) for x in (t, pn)), bef, hbm(go), *old)


def back(t, pr, g, aft, k, v, start, old):
    at = start // STEP
    return pl.pallas_call(
        back_kernel,
        out_shape=(shape(*k.shape), shape(*k.shape), shape(k.shape[1] // GSIZE, LN, kind=f32)),
        grid=(g.shape[1] // STEP,),
        in_specs=[table(B, at), table(H, at), tok(), tok(), tok(at), tok(at)] + [ANY] * len(old),
        out_specs=(tok(at), tok(at), table(1, at)),
        input_output_aliases={6 + i: i for i in range(len(old))},
        compiler_params=PARAMS,
        name="back",
    )(hbm(t), hbm(pr), hbm(g), aft, hbm(k), hbm(v), *old)


def pairs_of(size, step):
    return [(i, i ^ step) for i in range(size)]


def reduce_filter(partial, size):
    index = lax.axis_index("ctx")
    bits = size.bit_length() - 1
    order = [b for b in (2, 1) + tuple(range(3, bits)) + (0,) if b < bits]
    left = list(range(bits - 1, -1, -1))
    pieces = partial.reshape((2,) * bits + (partial.shape[0] // size, partial.shape[1]))
    for b in order:
        axis = left.index(b)
        bit = (index >> b) & 1
        keep = lax.dynamic_index_in_dim(pieces, bit, axis, keepdims=False)
        send = lax.dynamic_index_in_dim(pieces, 1 - bit, axis, keepdims=False)
        got = lax.ppermute(send, "ctx", pairs_of(size, 1 << b))
        pieces = keep + got
        left.remove(b)
    return pieces


PARTS = 2


def shards(query_rows, key_rows, value_rows, grad_out, conv_filter):
    size = lax.axis_size("ctx")
    channels = key_rows.shape[1]
    width = channels // PARTS
    down = [(i + 1, i) for i in range(size - 1)]
    up = [(i, i + 1) for i in range(size - 1)]
    gated, after = [], []
    for c in range(PARTS):
        cut = slice(c * width, (c + 1) * width)
        gated.append((grad_out[:, cut].astype(f32) * query_rows[:, cut].astype(f32)).astype(bf))
        after.append(lax.ppermute(gated[c], "ctx", down))
    product, pn, pr, tm, tb = prep(conv_filter, key_rows, value_rows)
    before = lax.ppermute(product, "ctx", up)
    old = ()
    for c in range(PARTS):
        old = back(tb, pr, gated[c], after[c], key_rows, value_rows, c * width, old)
    grad_key, grad_value, partial = old
    own = reduce_filter(partial, size)
    (grad_query,) = mixed(tm, pn, before, grad_out, 0, ())
    scale = 1.0 / math.sqrt(query_rows.shape[0] * size * GSIZE)
    return grad_query, grad_key, grad_value, own * scale


def solution(mesh):
    rows = P(("grp", "ctx"), None)

    return jax.shard_map(
        shards,
        mesh=mesh,
        in_specs=(rows, rows, rows, rows, P()),
        out_specs=(rows, rows, rows, rows),
        check_vma=False,
    )
```

```python
import math

import jax
import jax.numpy as jnp
from jax import lax
from jax.experimental import pallas as pl
from jax.experimental.pallas import tpu as pltpu
from jax.sharding import PartitionSpec as P

GSIZE = 16
f32 = jnp.float32
bf = jnp.bfloat16
LN = 128
B = 32
NB = LN // B
LB = LN // NB
SG = LB // GSIZE
GT = LN // GSIZE
H = 16
STEP = 1024
WIDE = 2048


def lanes(shape):
    return lax.broadcasted_iota(jnp.int32, shape, 1)


def subl(shape):
    return lax.broadcasted_iota(jnp.int32, shape, 0)


def network(vs):
    lane = lanes(vs[0].shape)
    cur = [vs[(-m) % NB] for m in range(NB)]
    bit = 1
    while bit < NB:
        mask = (lane & (bit * LB)) != 0
        cur = [jnp.where(mask, cur[(m - bit) % NB], cur[m]) for m in range(NB)]
        bit *= 2
    return cur


def rot(x, s):
    s %= LN
    return x if s == 0 else pltpu.roll(x, s, 1)


def to_groups(tile):
    return network([rot(tile[B * a : B * a + B, :], LB * a) for a in range(NB)])


def to_tokens(vs):
    return [rot(e, -LB * a) for a, e in enumerate(network(vs))]


def place(shape, s):
    return (lanes(shape) // LB - s) & (NB - 1)


def unfold_back(now, bef, s):
    blk = place(now.shape, s)
    mid = [rot(jnp.where(blk < NB - d, now, bef), LB * d) for d in range(NB - 1, 0, -1)]
    return jnp.concatenate([bef] + mid + [now], 0)


def unfold_fwd(now, aft, s):
    blk = place(now.shape, s)
    mid = [rot(jnp.where(blk >= d, now, aft), -LB * d) for d in range(1, NB)]
    return jnp.concatenate([now] + mid + [aft], 0)


def pick(out, half):
    lane = lanes((B, LN))
    y = out[half * SG * B : half * SG * B + B, half * LN : half * LN + LN]
    for q in range(1, SG):
        other = out[(half * SG + q) * B : (half * SG + q + 1) * B, half * LN : half * LN + LN]
        y = jnp.where((lane // GSIZE) % SG == q, other, y)
    return y


def column_sums(vs):
    row = subl(vs[0].shape)
    bit = 1
    while len(vs) > 1:
        low = (row & bit) == 0
        vs = [
            jnp.where(low, a, b) + pltpu.roll(jnp.where(low, b, a), 8 - bit, 0)
            for a, b in zip(vs[0::2], vs[1::2])
        ]
        bit *= 2
    return vs[0]


def prep_kernel(h_ref, k_ref, v_ref, p_ref, pn_ref, pr_ref, tm_ref, tb_ref):
    nt = k_ref.shape[1] // LN
    flip = jnp.where(lanes((H, H)) + subl((H, H)) == H - 1, 1.0, 0.0).astype(bf)
    turn = jnp.where(lanes((LN, LN)) + subl((LN, LN)) == LN - 1, 1.0, 0.0).astype(bf)
    h = h_ref[...].astype(f32)
    hr = jnp.dot(h_ref[...], turn, preferred_element_type=f32)
    for j in range(nt):
        co = slice(j * LN, (j + 1) * LN)
        p = (k_ref[:, co].astype(f32) * v_ref[:, co].astype(f32)).astype(bf)
        p_ref[:, co] = p
        ps = to_groups(p)
        for s in range(NB):
            r = (j * NB + s) * B
            pn_ref[r : r + B, :] = ps[s]
            for at in range(0, B, H):
                x = jnp.dot(flip, ps[s][at : at + H], preferred_element_type=f32)
                pr_ref[r + at : r + at + H, :] = x.astype(bf)
        for g in range(j * GT, (j + 1) * GT):
            r0 = slice(g * B, (g + 1) * B)
            rm = jnp.broadcast_to(hr[g : g + 1, :], (B, LN))
            tm_ref[r0, :] = pltpu.roll(rm, 1, 1, stride=1, stride_axis=0).astype(bf)
            rb = jnp.broadcast_to(h[g : g + 1, :], (B, LN))
            tb_ref[r0, :] = pltpu.roll(rb, 0, 1, stride=1, stride_axis=0).astype(bf)


def taps_of(ring, first):
    out = []
    for x in (ring[i : i + B] for i in range(0, ring.shape[0], B)):
        inside = lanes(x.shape) > subl(x.shape) if first else lanes(x.shape) >= subl(x.shape)
        zero = jnp.zeros_like(x)
        out.append(jnp.concatenate([jnp.where(inside, x, zero), jnp.where(inside, zero, x)[:, :B]], 1))
    return jnp.concatenate(out, 0)


def mixed_kernel(t_ref, pn_ref, bef_ref, go_ref, *rest):
    gq_ref = rest[-1]
    nt = bef_ref.shape[1] // LN
    for j in range(nt):
        co = slice(j * LN, (j + 1) * LN)
        bef = to_groups(bef_ref[:, co])
        ys = []
        for s in range(0, NB, 2):
            us = []
            for i in (0, 1):
                r = (j * NB + s + i) * B
                us.append(unfold_back(pn_ref[r : r + B, :], bef[s + i], s + i))
            r = (j * GT + s * SG) * B
            t = taps_of(t_ref[r : r + 2 * SG * B, :], True)
            y = jnp.dot(t, jnp.concatenate(us, 1), preferred_element_type=f32)
            ys += [pick(y, 0), pick(y, 1)]
        for a, y in enumerate(to_tokens(ys)):
            rows = slice(B * a, B * a + B)
            gq_ref[rows, co] = (go_ref[rows, co].astype(f32) * y).astype(bf)


def back_kernel(t_ref, pr_ref, g_ref, aft_ref, k_ref, v_ref, *rest):
    gk_ref, gv_ref, f_ref = rest[-3:]
    nt = aft_ref.shape[1] // LN
    lane, row = lanes((H, LN)), subl((H, LN))
    for j in range(nt):
        co = slice(j * LN, (j + 1) * LN)
        now, aft = to_groups(g_ref[:, co]), to_groups(aft_ref[:, co])
        ys, sums = [], []
        for s in range(0, NB, 2):
            us = [unfold_fwd(now[s + i], aft[s + i], s + i) for i in (0, 1)]
            r = (j * GT + s * SG) * B
            t = taps_of(t_ref[r : r + 2 * SG * B, :], False)
            y = jnp.dot(t, jnp.concatenate(us, 1), preferred_element_type=f32)
            ys += [pick(y, 0), pick(y, 1)]
            for i in (0, 1):
                r = (j * NB + s + i) * B
                rhs = jnp.concatenate([us[i][0 : LN + H], us[i][H : LN + 2 * H]], 1)
                own = jnp.concatenate([pr_ref[r : r + H, :], pr_ref[r + H : r + B, :]], 1)
                part = (lanes(own.shape) // GSIZE) % SG
                lhs = jnp.concatenate([jnp.where(part == q, own, jnp.zeros_like(own)) for q in range(SG)], 0)
                both = lax.dot_general(
                    lhs, rhs, (((1,), (1,)), ((), ())), preferred_element_type=f32
                )
                for q in range(SG):
                    f = both[q * H : (q + 1) * H]
                    edge = jnp.concatenate([f[:, LN : LN + H], jnp.zeros((H, LN - H), f32)], 1)
                    c = jnp.where(lane + row < H - 1, edge, f[:, :LN])
                    c = pltpu.roll(c, LN - H + 1, 1, stride=1, stride_axis=0)
                    sums.append(c[:8] + c[8:])
        f_ref[j * GT : (j + 1) * GT, :] = column_sums(sums)
        for a, y in enumerate(to_tokens(ys)):
            sl = (slice(B * a, B * a + B), co)
            gk_ref[sl] = (v_ref[sl].astype(f32) * y).astype(bf)
            gv_ref[sl] = (k_ref[sl].astype(f32) * y).astype(bf)


def hbm(x):
    return pltpu.with_memory_space_constraint(x, pltpu.HBM)


def tok(start=0):
    return pl.BlockSpec((LN, STEP), lambda i: (0, i + start))


def table(rows, start=0):
    return pl.BlockSpec((STEP // GSIZE * rows, LN), lambda i: (i + start, 0))


def shape(*dims, kind=bf):
    return jax.ShapeDtypeStruct(dims, kind)


def prep(h, k, v):
    groups = h.shape[0]
    t, r = shape(groups * B, LN), shape(groups * H, LN)
    return pl.pallas_call(
        prep_kernel,
        out_shape=(shape(*k.shape), r, r, t, t),
        grid=(k.shape[1] // STEP,),
        in_specs=[table(1), tok(), tok()],
        out_specs=(tok(), table(H), table(H), table(B), table(B)),
        name="prep",
    )(hbm(h), hbm(k), hbm(v))


ANY = pl.BlockSpec(memory_space=pl.ANY)
PARAMS = pltpu.CompilerParams(vmem_limit_bytes=48 << 20)


def block(ref, rows, step):
    if rows == 0:
        return ref.at[:, pl.ds(step * WIDE, WIDE)]
    height = WIDE // GSIZE * rows
    return ref.at[pl.ds(step * height, height), :]


def buffer(steps, rows, kind):
    dims = (LN, WIDE) if rows == 0 else (WIDE // GSIZE * rows, LN)
    return pltpu.VMEM((steps,) + dims, kind)


def streamed(compute, steps, ins, outs, old=(), limit=None):
    n_in, n_old, n_out = len(ins), len(old), len(outs)

    def kernel(*refs):
        sources, refs = refs[:n_in], refs[n_in + n_old :]
        targets, refs = refs[:n_out], refs[n_out:]
        held, refs = refs[:n_in], refs[n_in:]
        made, (in_sem, out_sem) = refs[:n_out], refs[n_out:]

        def load(i, c):
            source = block(sources[i], ins[i][1], ins[i][2] + c)
            return pltpu.make_async_copy(source, held[i].at[c], in_sem.at[i, c])

        def save(i, c):
            target = block(targets[i], outs[i][1], outs[i][2] + c)
            return pltpu.make_async_copy(made[i].at[c], target, out_sem.at[i, c])

        for c in range(steps):
            for i in range(n_in):
                load(i, c).start()

        def one(c, carry):
            for i in range(n_in):
                load(i, c).wait()
            compute(*(x.at[c] for x in held), *(x.at[c] for x in made))
            for i in range(n_out):
                save(i, c).start()
            return carry

        for c in range(steps):
            one(c, 0)
        for c in range(steps):
            for i in range(n_out):
                save(i, c).wait()

    anywhere = pl.BlockSpec(memory_space=pl.ANY)
    return pl.pallas_call(
        kernel,
        out_shape=tuple(x[0] for x in outs),
        in_specs=[anywhere] * (n_in + n_old),
        out_specs=(anywhere,) * n_out,
        scratch_shapes=[buffer(steps, x[1], x[0].dtype) for x in ins]
        + [buffer(steps, x[1], x[0].dtype) for x in outs]
        + [pltpu.SemaphoreType.DMA((n_in, steps)), pltpu.SemaphoreType.DMA((n_out, steps))],
        input_output_aliases={n_in + i: i for i in range(n_old)},
        compiler_params=pltpu.CompilerParams(vmem_limit_bytes=limit),
    )(*(x[0] if x[3] else hbm(x[0]) for x in ins), *old)


def mixed(t, pn, bef, go):
    return streamed(
        mixed_kernel,
        go.shape[1] // WIDE,
        [(t, B, 0, False), (pn, H, 0, False), (bef, 0, 0, True), (go, 0, 0, False)],
        [(shape(*go.shape), 0, 0)],
        (),
        48 << 20,
    )


def back(t, pr, g, aft, k, v, start, old):
    at = start // STEP
    return pl.pallas_call(
        back_kernel,
        out_shape=(shape(*k.shape), shape(*k.shape), shape(k.shape[1] // GSIZE, LN, kind=f32)),
        grid=(g.shape[1] // STEP,),
        in_specs=[table(B, at), table(H, at), tok(), tok(), tok(at), tok(at)] + [ANY] * len(old),
        out_specs=(tok(at), tok(at), table(1, at)),
        input_output_aliases={6 + i: i for i in range(len(old))},
        compiler_params=PARAMS,
        name="back",
    )(hbm(t), hbm(pr), hbm(g), aft, hbm(k), hbm(v), *old)


def pairs_of(size, step):
    return [(i, i ^ step) for i in range(size)]


def reduce_filter(partial, size):
    index = lax.axis_index("ctx")
    bits = size.bit_length() - 1
    order = [b for b in (2, 1) + tuple(range(3, bits)) + (0,) if b < bits]
    left = list(range(bits - 1, -1, -1))
    pieces = partial.reshape((2,) * bits + (partial.shape[0] // size, partial.shape[1]))
    for b in order:
        axis = left.index(b)
        bit = (index >> b) & 1
        keep = lax.dynamic_index_in_dim(pieces, bit, axis, keepdims=False)
        send = lax.dynamic_index_in_dim(pieces, 1 - bit, axis, keepdims=False)
        got = lax.ppermute(send, "ctx", pairs_of(size, 1 << b))
        pieces = keep + got
        left.remove(b)
    return pieces


PARTS = 2


def shards(query_rows, key_rows, value_rows, grad_out, conv_filter):
    size = lax.axis_size("ctx")
    channels = key_rows.shape[1]
    width = channels // PARTS
    down = [(i + 1, i) for i in range(size - 1)]
    up = [(i, i + 1) for i in range(size - 1)]
    gated, after = [], []
    for c in range(PARTS):
        cut = slice(c * width, (c + 1) * width)
        gated.append((grad_out[:, cut].astype(f32) * query_rows[:, cut].astype(f32)).astype(bf))
        after.append(lax.ppermute(gated[c], "ctx", down))
    product, pn, pr, tm, tb = prep(conv_filter, key_rows, value_rows)
    before = lax.ppermute(product, "ctx", up)
    old = ()
    for c in range(PARTS):
        old = back(tb, pr, gated[c], after[c], key_rows, value_rows, c * width, old)
    grad_key, grad_value, partial = old
    own = reduce_filter(partial, size)
    (grad_query,) = mixed(tm, pn, before, grad_out)
    scale = 1.0 / math.sqrt(query_rows.shape[0] * size * GSIZE)
    return grad_query, grad_key, grad_value, own * scale


def solution(mesh):
    rows = P(("grp", "ctx"), None)

    return jax.shard_map(
        shards,
        mesh=mesh,
        in_specs=(rows, rows, rows, rows, P()),
        out_specs=(rows, rows, rows, rows),
        check_vma=False,
    )
```

```python
import math

import jax
import jax.numpy as jnp
from jax import lax
from jax.experimental import pallas as pl
from jax.experimental.pallas import tpu as pltpu
from jax.sharding import PartitionSpec as P

GSIZE = 16
f32 = jnp.float32
bf = jnp.bfloat16
LN = 128
B = 32
NB = LN // B
LB = LN // NB
SG = LB // GSIZE
GT = LN // GSIZE
H = 16
STEP = 1024
WIDE = 2048


def lanes(shape):
    return lax.broadcasted_iota(jnp.int32, shape, 1)


def subl(shape):
    return lax.broadcasted_iota(jnp.int32, shape, 0)


def network(vs):
    lane = lanes(vs[0].shape)
    cur = [vs[(-m) % NB] for m in range(NB)]
    bit = 1
    while bit < NB:
        mask = (lane & (bit * LB)) != 0
        cur = [jnp.where(mask, cur[(m - bit) % NB], cur[m]) for m in range(NB)]
        bit *= 2
    return cur


def rot(x, s):
    s %= LN
    return x if s == 0 else pltpu.roll(x, s, 1)


def to_groups(tile):
    return network([rot(tile[B * a : B * a + B, :], LB * a) for a in range(NB)])


def to_tokens(vs):
    return [rot(e, -LB * a) for a, e in enumerate(network(vs))]


def place(shape, s):
    return (lanes(shape) // LB - s) & (NB - 1)


def unfold_back(now, bef, s):
    blk = place(now.shape, s)
    mid = [rot(jnp.where(blk < NB - d, now, bef), LB * d) for d in range(NB - 1, 0, -1)]
    return jnp.concatenate([bef] + mid + [now], 0)


def unfold_fwd(now, aft, s):
    blk = place(now.shape, s)
    mid = [rot(jnp.where(blk >= d, now, aft), -LB * d) for d in range(1, NB)]
    return jnp.concatenate([now] + mid + [aft], 0)


def pick(out, half):
    lane = lanes((B, LN))
    y = out[half * SG * B : half * SG * B + B, half * LN : half * LN + LN]
    for q in range(1, SG):
        other = out[(half * SG + q) * B : (half * SG + q + 1) * B, half * LN : half * LN + LN]
        y = jnp.where((lane // GSIZE) % SG == q, other, y)
    return y


def column_sums(vs):
    row = subl(vs[0].shape)
    bit = 1
    while len(vs) > 1:
        low = (row & bit) == 0
        vs = [
            jnp.where(low, a, b) + pltpu.roll(jnp.where(low, b, a), 8 - bit, 0)
            for a, b in zip(vs[0::2], vs[1::2])
        ]
        bit *= 2
    return vs[0]


def prep_kernel(h_ref, k_ref, v_ref, p_ref, pn_ref, pr_ref, tm_ref, tb_ref):
    nt = k_ref.shape[1] // LN
    flip = jnp.where(lanes((H, H)) + subl((H, H)) == H - 1, 1.0, 0.0).astype(bf)
    turn = jnp.where(lanes((LN, LN)) + subl((LN, LN)) == LN - 1, 1.0, 0.0).astype(bf)
    h = h_ref[...].astype(f32)
    hr = jnp.dot(h_ref[...], turn, preferred_element_type=f32)
    for j in range(nt):
        co = slice(j * LN, (j + 1) * LN)
        p = (k_ref[:, co].astype(f32) * v_ref[:, co].astype(f32)).astype(bf)
        p_ref[:, co] = p
        ps = to_groups(p)
        for s in range(NB):
            r = (j * NB + s) * B
            pn_ref[r : r + B, :] = ps[s]
            for at in range(0, B, H):
                x = jnp.dot(flip, ps[s][at : at + H], preferred_element_type=f32)
                pr_ref[r + at : r + at + H, :] = x.astype(bf)
        for g in range(j * GT, (j + 1) * GT):
            r0 = slice(g * B, (g + 1) * B)
            rm = jnp.broadcast_to(hr[g : g + 1, :], (B, LN))
            tm_ref[r0, :] = pltpu.roll(rm, 1, 1, stride=1, stride_axis=0).astype(bf)
            rb = jnp.broadcast_to(h[g : g + 1, :], (B, LN))
            tb_ref[r0, :] = pltpu.roll(rb, 0, 1, stride=1, stride_axis=0).astype(bf)


def taps_of(ring, first):
    out = []
    for x in (ring[i : i + B] for i in range(0, ring.shape[0], B)):
        inside = lanes(x.shape) > subl(x.shape) if first else lanes(x.shape) >= subl(x.shape)
        zero = jnp.zeros_like(x)
        out.append(jnp.concatenate([jnp.where(inside, x, zero), jnp.where(inside, zero, x)[:, :B]], 1))
    return jnp.concatenate(out, 0)


def mixed_kernel(t_ref, pn_ref, bef_ref, go_ref, *rest):
    gq_ref = rest[-1]
    nt = bef_ref.shape[1] // LN
    for j in range(nt):
        co = slice(j * LN, (j + 1) * LN)
        bef = to_groups(bef_ref[:, co])
        ys = []
        for s in range(0, NB, 2):
            us = []
            for i in (0, 1):
                r = (j * NB + s + i) * B
                us.append(unfold_back(pn_ref[r : r + B, :], bef[s + i], s + i))
            r = (j * GT + s * SG) * B
            t = taps_of(t_ref[r : r + 2 * SG * B, :], True)
            y = jnp.dot(t, jnp.concatenate(us, 1), preferred_element_type=f32)
            ys += [pick(y, 0), pick(y, 1)]
        for a, y in enumerate(to_tokens(ys)):
            rows = slice(B * a, B * a + B)
            gq_ref[rows, co] = (go_ref[rows, co].astype(f32) * y).astype(bf)


def back_kernel(refs, sums_too, rows_too):
    if rows_too:
        t_ref, refs = refs[0], refs[1:]
    if sums_too:
        pr_ref, refs = refs[0], refs[1:]
    g_ref, aft_ref = refs[:2]
    if rows_too:
        k_ref, v_ref = refs[2:4]
        gk_ref, gv_ref = refs[-3:-1] if sums_too else refs[-2:]
    if sums_too:
        f_ref = refs[-1]
    nt = aft_ref.shape[1] // LN
    lane, row = lanes((H, LN)), subl((H, LN))
    for j in range(nt):
        co = slice(j * LN, (j + 1) * LN)
        now, aft = to_groups(g_ref[:, co]), to_groups(aft_ref[:, co])
        ys, sums = [], []
        for s in range(0, NB, 2):
            us = [unfold_fwd(now[s + i], aft[s + i], s + i) for i in (0, 1)]
            if rows_too:
                r = (j * GT + s * SG) * B
                t = taps_of(t_ref[r : r + 2 * SG * B, :], False)
                y = jnp.dot(t, jnp.concatenate(us, 1), preferred_element_type=f32)
                ys += [pick(y, 0), pick(y, 1)]
            for i in (0, 1) if sums_too else ():
                r = (j * NB + s + i) * B
                rhs = jnp.concatenate([us[i][0 : LN + H], us[i][H : LN + 2 * H]], 1)
                own = jnp.concatenate([pr_ref[r : r + H, :], pr_ref[r + H : r + B, :]], 1)
                part = (lanes(own.shape) // GSIZE) % SG
                lhs = jnp.concatenate([jnp.where(part == q, own, jnp.zeros_like(own)) for q in range(SG)], 0)
                both = lax.dot_general(
                    lhs, rhs, (((1,), (1,)), ((), ())), preferred_element_type=f32
                )
                for q in range(SG):
                    f = both[q * H : (q + 1) * H]
                    edge = jnp.concatenate([f[:, LN : LN + H], jnp.zeros((H, LN - H), f32)], 1)
                    c = jnp.where(lane + row < H - 1, edge, f[:, :LN])
                    c = pltpu.roll(c, LN - H + 1, 1, stride=1, stride_axis=0)
                    sums.append(c[:8] + c[8:])
        if sums_too:
            f_ref[j * GT : (j + 1) * GT, :] = column_sums(sums)
        for a, y in enumerate(to_tokens(ys)) if rows_too else ():
            sl = (slice(B * a, B * a + B), co)
            gk_ref[sl] = (v_ref[sl].astype(f32) * y).astype(bf)
            gv_ref[sl] = (k_ref[sl].astype(f32) * y).astype(bf)


def hbm(x):
    return pltpu.with_memory_space_constraint(x, pltpu.HBM)


def tok(start=0):
    return pl.BlockSpec((LN, STEP), lambda i: (0, i + start))


def table(rows, start=0):
    return pl.BlockSpec((STEP // GSIZE * rows, LN), lambda i: (i + start, 0))


def shape(*dims, kind=bf):
    return jax.ShapeDtypeStruct(dims, kind)


def prep(h, k, v):
    groups = h.shape[0]
    t, r = shape(groups * B, LN), shape(groups * H, LN)
    return pl.pallas_call(
        prep_kernel,
        out_shape=(shape(*k.shape), r, r, t, t),
        grid=(k.shape[1] // STEP,),
        in_specs=[table(1), tok(), tok()],
        out_specs=(tok(), table(H), table(H), table(B), table(B)),
        name="prep",
    )(hbm(h), hbm(k), hbm(v))


ANY = pl.BlockSpec(memory_space=pl.ANY)
PARAMS = pltpu.CompilerParams(vmem_limit_bytes=48 << 20)


def block(ref, rows, step):
    if rows == 0:
        return ref.at[:, pl.ds(step * WIDE, WIDE)]
    height = WIDE // GSIZE * rows
    return ref.at[pl.ds(step * height, height), :]


def buffer(steps, rows, kind):
    dims = (LN, WIDE) if rows == 0 else (WIDE // GSIZE * rows, LN)
    return pltpu.VMEM((steps,) + dims, kind)


def streamed(compute, steps, ins, outs, old=(), limit=None):
    n_in, n_old, n_out = len(ins), len(old), len(outs)

    def kernel(*refs):
        sources, refs = refs[:n_in], refs[n_in + n_old :]
        targets, refs = refs[:n_out], refs[n_out:]
        held, refs = refs[:n_in], refs[n_in:]
        made, (in_sem, out_sem) = refs[:n_out], refs[n_out:]

        def load(i, c):
            source = block(sources[i], ins[i][1], ins[i][2] + c)
            return pltpu.make_async_copy(source, held[i].at[c], in_sem.at[i, c])

        def save(i, c):
            target = block(targets[i], outs[i][1], outs[i][2] + c)
            return pltpu.make_async_copy(made[i].at[c], target, out_sem.at[i, c])

        for c in range(steps):
            for i in range(n_in):
                load(i, c).start()

        def one(c, carry):
            for i in range(n_in):
                load(i, c).wait()
            compute(*(x.at[c] for x in held), *(x.at[c] for x in made))
            for i in range(n_out):
                save(i, c).start()
            return carry

        for c in range(steps):
            one(c, 0)
        for c in range(steps):
            for i in range(n_out):
                save(i, c).wait()

    anywhere = pl.BlockSpec(memory_space=pl.ANY)
    return pl.pallas_call(
        kernel,
        out_shape=tuple(x[0] for x in outs),
        in_specs=[anywhere] * (n_in + n_old),
        out_specs=(anywhere,) * n_out,
        scratch_shapes=[buffer(steps, x[1], x[0].dtype) for x in ins]
        + [buffer(steps, x[1], x[0].dtype) for x in outs]
        + [pltpu.SemaphoreType.DMA((n_in, steps)), pltpu.SemaphoreType.DMA((n_out, steps))],
        input_output_aliases={n_in + i: i for i in range(n_old)},
        compiler_params=pltpu.CompilerParams(vmem_limit_bytes=limit),
    )(*(x[0] if x[3] else hbm(x[0]) for x in ins), *old)


def mixed(t, pn, bef, go):
    return streamed(
        mixed_kernel,
        go.shape[1] // WIDE,
        [(t, B, 0, False), (pn, H, 0, False), (bef, 0, 0, True), (go, 0, 0, False)],
        [(shape(*go.shape), 0, 0)],
        (),
        48 << 20,
    )


def back(t, pr, g, aft, k, v, start, old, sums_too=True, rows_too=True):
    at = start // STEP
    ins = [(hbm(t), table(B, at))] if rows_too else []
    ins += [(hbm(pr), table(H, at))] if sums_too else []
    ins += [(hbm(g), tok()), (aft, tok())]
    ins += [(hbm(k), tok(at)), (hbm(v), tok(at))] if rows_too else []
    outs = [(shape(*k.shape), tok(at))] * 2 if rows_too else []
    if sums_too:
        outs += [(shape(k.shape[1] // GSIZE, LN, kind=f32), table(1, at))]
    count = len(ins)
    ins += [(x, ANY) for x in old]
    return pl.pallas_call(
        lambda *refs: back_kernel(refs, sums_too, rows_too),
        out_shape=tuple(x[0] for x in outs),
        grid=(g.shape[1] // STEP,),
        in_specs=[x[1] for x in ins],
        out_specs=tuple(x[1] for x in outs),
        input_output_aliases={count + i: i for i in range(len(old))},
        compiler_params=PARAMS,
        name="back",
    )(*(x[0] for x in ins))


def pairs_of(size, step):
    return [(i, i ^ step) for i in range(size)]


def reduce_filter(partial, size):
    index = lax.axis_index("ctx")
    bits = size.bit_length() - 1
    order = [b for b in (2, 1) + tuple(range(3, bits)) + (0,) if b < bits]
    left = list(range(bits - 1, -1, -1))
    pieces = partial.reshape((2,) * bits + (partial.shape[0] // size, partial.shape[1]))
    for b in order:
        axis = left.index(b)
        bit = (index >> b) & 1
        keep = lax.dynamic_index_in_dim(pieces, bit, axis, keepdims=False)
        send = lax.dynamic_index_in_dim(pieces, 1 - bit, axis, keepdims=False)
        got = lax.ppermute(send, "ctx", pairs_of(size, 1 << b))
        pieces = keep + got
        left.remove(b)
    return pieces


PARTS = 2


def shards(query_rows, key_rows, value_rows, grad_out, conv_filter):
    size = lax.axis_size("ctx")
    channels = key_rows.shape[1]
    width = channels // PARTS
    down = [(i + 1, i) for i in range(size - 1)]
    up = [(i, i + 1) for i in range(size - 1)]
    gated, after = [], []
    for c in range(PARTS):
        cut = slice(c * width, (c + 1) * width)
        gated.append((grad_out[:, cut].astype(f32) * query_rows[:, cut].astype(f32)).astype(bf))
        after.append(lax.ppermute(gated[c], "ctx", down))
    product, pn, pr, tm, tb = prep(conv_filter, key_rows, value_rows)
    before = lax.ppermute(product, "ctx", up)

    def run(c, old, *kinds):
        return back(tb, pr, gated[c], after[c], key_rows, value_rows, c * width, old, *kinds)

    grad_key, grad_value, partial = run(0, ())
    (partial,) = run(1, (partial,), True, False)
    own = reduce_filter(partial, size)
    grad_key, grad_value = run(1, (grad_key, grad_value), False, True)
    (grad_query,) = mixed(tm, pn, before, grad_out)
    scale = 1.0 / math.sqrt(query_rows.shape[0] * size * GSIZE)
    return grad_query, grad_key, grad_value, own * scale


def solution(mesh):
    rows = P(("grp", "ctx"), None)

    return jax.shard_map(
        shards,
        mesh=mesh,
        in_specs=(rows, rows, rows, rows, P()),
        out_specs=(rows, rows, rows, rows),
        check_vma=False,
    )
```
